32 devices in a mesh: dp: 4 (over z), row: 4 (over y, core), col: 2 (over x).
Axes of the slice: x: 2, y: 2, z: 4, core: 2. Of those that a mesh axis runs over, the one named last changes fastest.
Arguments:
- tokens: bfloat16 [4096, 1024], P(('dp', 'col'), 'row'), may hold values from -6 to 6
- first_gain: float32 [1024], P('row'), may hold values from 0.25 to 1.75
- first_shift: float32 [1024], P('row'), may hold values from -1.75 to 1.75
- second_gain: float32 [1024], P('row'), may hold values from 0.25 to 1.75
- second_shift: float32 [1024], P('row'), may hold values from -1.75 to 1.75
- mixing_weight: bfloat16 [1024, 3072], P('row', 'col'), may hold values from -0.1875 to 0.1875
- mixing_bias: float32 [3072], P('col'), may hold values from -3 to 3
- output_weight: bfloat16 [1024, 1024], P('col', 'row'), may hold values from -1 to 1
- expand_weight: bfloat16 [1024, 4096], P('row', 'col'), may hold values from -0.1875 to 0.1875
- expand_bias: float32 [4096], P('col'), may hold values from -3 to 3
- shrink_weight: bfloat16 [4096, 1024], P('col', 'row'), may hold values from -0.09375 to 0.09375
- output_bias: float32 [1024], P('row'), may hold values from -3 to 3
- cotangent: bfloat16 [4096, 1024], P(('dp', 'col'), 'row'), may hold values from -8 to 8
Outputs:
- layer_out: bfloat16 [4096, 1024], P(('dp', 'col'), 'row')
- tokens_grad: float32 [4096, 1024], P(('dp', 'col'), 'row')
- first_gain_grad: float32 [1024], P(('row', 'dp'))
- first_shift_grad: float32 [1024], P(('row', 'dp'))
- second_gain_grad: float32 [1024], P(('row', 'dp'))
- second_shift_grad: float32 [1024], P(('row', 'dp'))
- mixing_weight_grad: float32 [1024, 3072], P(('row', 'dp'), 'col')
- mixing_bias_grad: float32 [3072], P(('col', 'dp'))
- output_weight_grad: float32 [1024, 1024], P(('col', 'dp'), 'row')
- expand_weight_grad: float32 [1024, 4096], P(('row', 'dp'), 'col')
- expand_bias_grad: float32 [4096], P(('col', 'dp'))
- shrink_weight_grad: float32 [4096, 1024], P(('col', 'dp'), 'row')
- output_bias_grad: float32 [1024], P(('row', 'dp'))
The draws below stay inside these ranges and needn't reach their ends.
All inputs are finite; a program needn't handle non-finite values.
Results may differ from the reference program's by a relative error of at most 0.015.
Values may be sent and summed in bfloat16 or wider, within the bound.
A program may use at most 128 MiB of HBM per device.

```python
import math
import jax
import jax.numpy as jnp
from jax import lax

D = 1024
HEADS = 16
FF = 4096
HEAD_DIM = 64
ROTARY = 16
SEQ = 1024
TOKENS = 4096
N_DP = 4


def raised(entries, own_key, source, target, blocks, factor):
    def block_of(axis_at):
        return (jnp.arange(entries.shape[axis_at]) // (entries.shape[axis_at] // blocks)).reshape((-1,) + (1,) * (entries.ndim - 1 - axis_at))

    one_side = jax.random.permutation(own_key, blocks)[block_of(target)]
    other_side = (block_of(target) + blocks // 2) % blocks
    return jnp.where((block_of(source) == one_side) | (block_of(source) == other_side), factor * entries, entries)


def block_scale(own_key, dims, shards, low, top_value):
    factor_of, own = 1.0, jax.random.fold_in(own_key, 6)
    for position, blocks in shards:
        steps = jnp.exp(jax.random.uniform(jax.random.fold_in(own, position), (blocks,), jnp.float32, low / len(shards), top_value / len(shards)))
        factor_of = factor_of * jnp.repeat(steps, dims[position] // blocks).reshape([-1 if axis == position else 1 for axis in range(len(dims))])
    return factor_of


def normal_values(rng, shape, scale, bound, split=(), held_as=jnp.bfloat16):
    loudness = block_scale(rng, shape, split, -0.22, 0.18) if split else 1.0
    array = jax.random.normal(rng, shape, jnp.float32) * scale * loudness
    return jnp.minimum(jnp.maximum(array, -bound), bound).astype(held_as)


def bell_draw_with(rng, shape, width, limit, split, heavy, kind=jnp.bfloat16):
    entries = width * jax.random.normal(rng, shape, jnp.float32)
    if split:
        entries = entries * block_scale(rng, shape, split, -0.22, 0.18)
    return jnp.clip(raised(entries, jax.random.fold_in(rng, 3), *heavy), -limit, limit).astype(kind)


def setup_inputs(seed: int = 0) -> dict:
    key_of = jax.random.split(jax.random.key(seed), 14)
    return {
        "tokens": normal_values(key_of[0], (TOKENS, D), 1.0, 6.0, ((0, 8), (1, 4))),
        "first_gain": jnp.clip(1.0 + 0.15 * jax.random.normal(key_of[1], (D,), jnp.float32), 0.25, 1.75),
        "first_shift": normal_values(key_of[2], (D,), 0.3, 1.75, ((0, 4),), jnp.float32),
        "second_gain": jnp.clip(1.0 + 0.15 * jax.random.normal(key_of[3], (D,), jnp.float32), 0.25, 1.75),
        "second_shift": normal_values(key_of[4], (D,), 0.3, 1.75, ((0, 4),), jnp.float32),
        "mixing_weight": normal_values(key_of[5], (D, 3 * D), D ** -0.5, 0.1875, ((0, 4), (1, 2))),
        "mixing_bias": normal_values(key_of[6], (3 * D,), 0.5, 3.0, ((0, 2),), jnp.float32),
        "output_weight": normal_values(key_of[7], (D, D), (D // 32) ** -0.5, 1.0, ((0, 2), (1, 4))),
        "expand_weight": normal_values(key_of[8], (D, FF), D ** -0.5, 0.1875, ((0, 4), (1, 2))),
        "expand_bias": normal_values(key_of[9], (FF,), 0.5, 3.0, ((0, 2),), jnp.float32),
        "shrink_weight": normal_values(key_of[10], (FF, D), FF ** -0.5, 0.09375, ((0, 2), (1, 4))),
        "output_bias": normal_values(key_of[11], (D,), 0.5, 3.0, ((0, 4),), jnp.float32),
        "cotangent": bell_draw_with(key_of[12], (TOKENS, D), 1.0, 8.0, ((0, 8), (1, 4)), (0, 1, 8, 2.0)),
    }


EPSILON = 1e-05
NEGATIVE = -1e+30

@jax.custom_vjp
def low(v):
    return lax.optimization_barrier(v.astype(jnp.bfloat16)).astype(jnp.float32)

@jax.custom_vjp
def low_back(v):
    return v

def low_keep(v):
    return (low(v), None)

def low_pass(kept, grad):
    return (grad,)

def back_keep(v):
    return (v, None)

def back_low(kept, grad):
    return (low(grad),)
low.defvjp(low_keep, low_pass)
low_back.defvjp(back_keep, back_low)

def rotary_tables(positions):
    ladder = jnp.arange(0, ROTARY // 2, dtype=jnp.float32)
    rotation_rates = 1.0 / 10000.0 ** (2.0 * ladder / ROTARY)
    angles = positions.astype(jnp.float32)[:, None] * rotation_rates[None, :]
    return (jnp.cos(angles)[:, None, :], jnp.sin(angles)[:, None, :])

def rotate(vectors, cosines, sine_values):
    half_dims = ROTARY // 2
    upper_part = vectors[..., :half_dims]
    lower_part = vectors[..., half_dims:ROTARY]
    remain_part = vectors[..., ROTARY:]
    return jnp.concatenate([upper_part * cosines - lower_part * sine_values, lower_part * cosines + upper_part * sine_values, remain_part], axis=-1)

def layer(inputs, params):
    first_gain, first_shift, second_gain, second_shift, mixing_weight, mixing_bias, output_weight, expand_weight, expand_bias, shrink_weight, output_bias = params
    highest = lax.Precision.HIGHEST
    center = inputs - lax.optimization_barrier(jnp.mean(inputs, axis=-1, keepdims=True))
    spread = lax.optimization_barrier(jnp.mean(center * center, axis=-1, keepdims=True))
    normal = center * lax.rsqrt(spread + EPSILON)
    first_in = low(normal * first_gain + first_shift)
    second_in = low(normal * second_gain + second_shift)
    projected = low_back(jnp.dot(first_in, mixing_weight, precision=highest) + mixing_bias)
    projected = projected.reshape(SEQ, HEADS, 3, HEAD_DIM)
    positions = jnp.arange(SEQ)
    cosines, sine_values = rotary_tables(positions)
    queries = low(rotate(projected[:, :, 0], cosines, sine_values))
    keys_all = low(rotate(projected[:, :, 1], cosines, sine_values))
    values_all = low(projected[:, :, 2])
    scores = jnp.einsum('qhd,khd->hqk', queries, keys_all, precision=highest) * (1.0 / math.sqrt(HEAD_DIM))
    scores = low_back(scores)
    causal = positions[:, None] >= positions[None, :]
    scores = jnp.where(causal[None], scores, NEGATIVE)
    weights_low = low(jax.nn.softmax(scores, axis=-1))
    attended = jnp.einsum('hqk,khd->qhd', weights_low, values_all, precision=highest)
    attended = low(low_back(attended)).reshape(SEQ, D)
    expanded = low_back(jnp.dot(second_in, expand_weight, precision=highest) + expand_bias)
    activated = low(jax.nn.gelu(expanded, approximate=False))
    branch = jnp.dot(attended, output_weight, precision=highest) + jnp.dot(activated, shrink_weight, precision=highest)
    return inputs + branch + output_bias

def reference(tokens, first_gain, first_shift, second_gain, second_shift, mixing_weight, mixing_bias, output_weight, expand_weight, expand_bias, shrink_weight, output_bias, cotangent):
    params = tuple((weight.astype(jnp.float32) for weight in (first_gain, first_shift, second_gain, second_shift, mixing_weight, mixing_bias, output_weight, expand_weight, expand_bias, shrink_weight, output_bias)))
    inputs = tokens.astype(jnp.float32).reshape(N_DP, SEQ, D)
    cotangents = cotangent.astype(jnp.float32).reshape(N_DP, SEQ, D)
    zeroed = jax.tree.map(jnp.zeros_like, params)

    def advance(running, couple):
        seq_inputs, seq_cotangent = couple
        result, pullback = jax.vjp(layer, seq_inputs, params)
        input_grad, param_grads = pullback(seq_cotangent)
        running = jax.tree.map(lambda summed, addend: summed + addend, running, param_grads)
        return (running, (result.astype(jnp.bfloat16), input_grad))
    totals, (outputs, input_grads) = lax.scan(advance, zeroed, (inputs, cotangents))
    return (outputs.reshape(TOKENS, D), input_grads.reshape(TOKENS, D), totals[0], totals[1], totals[2], totals[3], totals[4], totals[5], totals[6], totals[7], totals[8], totals[9], totals[10])
```

```python
import functools
import math

import jax
import jax.numpy as jnp
from jax import lax
from jax.experimental import pallas as pl
from jax.experimental.pallas import tpu as pltpu
from jax.sharding import PartitionSpec as P

D = 1024
HEAD_DIM = 64
ROTARY = 16


EPSILON = 1e-05
NEGATIVE = -1e30


def rotary_tables(positions):
    ladder = jnp.arange(0, ROTARY // 2, dtype=jnp.float32)
    rotation_rates = 1.0 / 10000.0 ** (2.0 * ladder / ROTARY)
    angles = positions.astype(jnp.float32)[:, None] * rotation_rates[None, :]
    return (jnp.cos(angles)[:, None, :], jnp.sin(angles)[:, None, :])


def rotate(vectors, cosines, sine_values):
    half_dims = ROTARY // 2
    upper_part = vectors[..., :half_dims]
    lower_part = vectors[..., half_dims:ROTARY]
    remain_part = vectors[..., ROTARY:]
    return jnp.concatenate(
        [
            upper_part * cosines - lower_part * sine_values,
            lower_part * cosines + upper_part * sine_values,
            remain_part,
        ],
        axis=-1,
    )


def unrotate(gradient, cosines, sine_values):
    half_dims = ROTARY // 2
    upper_part = gradient[..., :half_dims]
    lower_part = gradient[..., half_dims:ROTARY]
    remain_part = gradient[..., ROTARY:]
    return jnp.concatenate(
        [
            upper_part * cosines + lower_part * sine_values,
            lower_part * cosines - upper_part * sine_values,
            remain_part,
        ],
        axis=-1,
    )


MESH = pl.DeviceIdType.MESH


def contract_rows(left_side, right_side):
    return lax.dot_general(
        left_side, right_side, (((0,), (0,)), ((), ())), preferred_element_type=jnp.float32
    )


def contract_cols(left_side, right_side):
    return lax.dot_general(
        left_side, right_side, (((1,), (1,)), ((), ())), preferred_element_type=jnp.float32
    )


def exact_gelu(values):
    return jax.nn.gelu(values, approximate=False)


def piece_of(ref, kind, index):
    if kind == "lanes":
        width = ref.shape[1] // 4
        return ref.at[:, pl.ds(pl.multiple_of(index * width, 128), width)]
    if kind == "whole":
        return ref
    return ref.at[index]


def place_of(ref, kind, index):
    if kind == "cols":
        width = ref.shape[1] // 4
        return ref.at[:, pl.ds(pl.multiple_of(index * width, 128), width)]
    height = ref.shape[0] // 4
    return ref.at[pl.ds(pl.multiple_of(index * height, 8), height)]


def exchange_kernel(n_gather, kinds, *refs):
    n_in = n_gather + len(kinds)
    sources, targets = refs[:n_in], refs[n_in : 2 * n_in]
    send_sems, recv_sems, own_sems = refs[2 * n_in :]
    r, c = lax.axis_index("row"), lax.axis_index("col")
    across = lax.rem(r + 2, 4)
    mate = r + 1 - 2 * lax.rem(r, 2)
    other = 1 - c
    barrier = pltpu.get_barrier_semaphore()
    peers = [(lax.rem(r + s, 4), c) for s in (1, 2, 3)]
    if n_gather:
        peers += [(r, other), (across, other)]
    for row, col in peers:
        pl.semaphore_signal(
            barrier, inc=1, device_id={"row": row, "col": col}, device_id_type=MESH
        )
    pl.semaphore_wait(barrier, len(peers))

    counter = [0]

    def send(src, dst, row, col):
        k = counter[0]
        counter[0] += 1
        copy = pltpu.make_async_remote_copy(
            src_ref=src,
            dst_ref=dst,
            send_sem=send_sems.at[k],
            recv_sem=recv_sems.at[k],
            device_id={"row": row, "col": col},
            device_id_type=MESH,
        )
        copy.start()
        return copy

    def block_at(ref, row, col):
        height, width = ref.shape[0] // 2, ref.shape[1] // 4
        return ref.at[
            pl.ds(pl.multiple_of(col * height, 8), height),
            pl.ds(pl.multiple_of(row * width, 128), width),
        ]

    owns, first, rest = [], [], []
    for g in range(n_gather):
        for row, col in ((across, c), (r, other), (across, other)):
            first.append((g, row, col, send(sources[g], block_at(targets[g], r, c), row, col)))
    for g in range(n_gather):
        rest.append(send(sources[g], block_at(targets[g], r, c), mate, c))
    for t, kind in enumerate(kinds):
        for shift in (2, 3, 1):
            peer = lax.rem(r + shift, 4)
            rest.append(
                send(
                    piece_of(sources[n_gather + t], kind, peer),
                    place_of(targets[n_gather + t], kind, r),
                    peer,
                    c,
                )
            )
    for t in range(n_in):
        if t < n_gather:
            src, dst = sources[t], block_at(targets[t], r, c)
        else:
            kind = kinds[t - n_gather]
            src, dst = piece_of(sources[t], kind, r), place_of(targets[t], kind, r)
        copy = pltpu.make_async_copy(src, dst, own_sems.at[t])
        copy.start()
        owns.append(copy)
    for g, row, col, copy in first:
        copy.wait_recv()
        spot = block_at(targets[g], row, col)
        rest.append(send(spot, spot, mate, c))
    for g, row, col, copy in first:
        copy.wait_send()
    for copy in rest:
        copy.wait()
    for copy in owns:
        copy.wait()


def exchange(gathers, moves, number):
    kinds = tuple(kind for kind, _ in moves)
    operands = tuple(gathers) + tuple(array for _, array in moves)
    outs = [jax.ShapeDtypeStruct((a.shape[0] * 2, a.shape[1] * 4), a.dtype) for a in gathers]
    for kind, a in moves:
        if kind == "lanes":
            shape = (a.shape[0] * 4, a.shape[1] // 4)
        elif kind == "whole":
            shape = (a.shape[0] * 4, a.shape[1])
        elif kind == "rows":
            shape = (a.shape[1] * 4, a.shape[2])
        else:
            shape = (a.shape[1], a.shape[2] * 4)
        outs.append(jax.ShapeDtypeStruct(shape, a.dtype))
    copies = 7 * len(gathers) + 3 * len(moves)
    return pl.pallas_call(
        functools.partial(exchange_kernel, len(gathers), kinds),
        out_shape=outs,
        in_specs=[pl.BlockSpec(memory_space=pltpu.VMEM)] * len(operands),
        out_specs=[pl.BlockSpec(memory_space=pltpu.VMEM)] * len(operands),
        scratch_shapes=[
            pltpu.SemaphoreType.DMA((copies,)),
            pltpu.SemaphoreType.DMA((copies,)),
            pltpu.SemaphoreType.DMA((len(operands),)),
        ],
        compiler_params=pltpu.CompilerParams(collective_id=number, has_side_effects=True),
    )(*operands)


def take(array, index, axis):
    return lax.dynamic_index_in_dim(array, index, axis, keepdims=False)


def plane_scatter(partial, r, c):
    n_row, n_col = 4, 2
    blocks = partial.astype(jnp.bfloat16).reshape(2, partial.shape[0] // 2, 2, 2, -1)
    core, y = r % 2, r // 2
    got = lax.ppermute(take(blocks, 1 - core, 3), "row", [(i, i ^ 1) for i in range(n_row)])
    both = take(blocks, core, 3).astype(jnp.float32) + got.astype(jnp.float32)
    low = both.astype(jnp.bfloat16)
    total = take(take(both, c, 0), y, 1)
    for dy, dc in ((1, 1), (1, 0), (0, 1)):
        sent = take(take(low, (c + dc) % 2, 0), (y + dy) % 2, 1)
        pairs = [
            (i * n_col + j, (i ^ (2 * dy)) * n_col + (j ^ dc))
            for i in range(n_row)
            for j in range(n_col)
        ]
        total = total + lax.ppermute(sent, ("row", "col"), pairs).astype(jnp.float32)
    return total


def dp_scatter(chunks, n_dp, d):
    if n_dp > 8:
        return lax.psum_scatter(chunks.astype(jnp.bfloat16), "dp", scatter_dimension=0).astype(
            jnp.float32
        )
    low = chunks.astype(jnp.bfloat16)
    total = take(chunks, d, 0).astype(jnp.float32)
    for shift in range(1, n_dp):
        sent = take(low, (d + shift) % n_dp, 0)
        pairs = [(i, (i + shift) % n_dp) for i in range(n_dp)]
        total = total + lax.ppermute(sent, "dp", pairs).astype(jnp.float32)
    return total


def row_swap(chunks, r):
    low = chunks.astype(jnp.bfloat16)
    result = low
    for shift in (1, 2, 3):
        sent = take(low, (r + shift) % 4, 0)
        came = lax.ppermute(sent, "row", [(i, (i + shift) % 4) for i in range(4)])
        result = lax.dynamic_update_index_in_dim(result, came, (r - shift) % 4, 0)
    return result


def body(
    tokens,
    first_gain,
    first_shift,
    second_gain,
    second_shift,
    mixing_weight,
    mixing_bias,
    output_weight,
    expand_weight,
    expand_bias,
    shrink_weight,
    output_bias,
    cotangent,
):
    n_dp = lax.axis_size("dp")
    d, r, c = lax.axis_index("dp"), lax.axis_index("row"), lax.axis_index("col")
    ff_block = expand_weight.shape[1] // 4
    unit = ff_block // n_dp

    def by_unit(array, axis):
        dims = array.shape
        split = array.reshape(dims[:axis] + (n_dp, 4, unit) + dims[axis + 1 :])
        moved = jnp.moveaxis(split, axis + 1, 0)
        return moved.reshape((4,) + dims[:axis] + (ff_block,) + dims[axis + 1 :])

    vectors = jnp.stack([first_gain, first_shift, second_gain, second_shift])
    vectors = jnp.concatenate([vectors, jnp.zeros_like(vectors)])
    tokens_all, mixing_all, vectors_all = exchange(
        [tokens], [("lanes", mixing_weight), ("whole", vectors)], 0
    )
    cotangent_all, expand_all, shrink_all, output_all = exchange(
        [cotangent],
        [
            ("rows", by_unit(expand_weight, 1)),
            ("cols", by_unit(shrink_weight, 0)),
            ("cols", output_weight.reshape(4, -1, output_weight.shape[1])),
        ],
        1,
    )
    vectors_all = vectors_all.reshape(4, 8, -1).transpose(1, 0, 2).reshape(8, -1)
    gain_one, shift_one, gain_two, shift_two = (vectors_all[i] for i in range(4))
    mixing_own = take(mixing_bias.reshape(4, -1), r, 0)
    expand_own = take(by_unit(expand_bias, 0), r, 0)

    seq_len = tokens_all.shape[0]
    floats = tokens_all.astype(jnp.float32)
    center = floats - jnp.mean(floats, axis=1, keepdims=True)
    inverse = lax.rsqrt(jnp.mean(center * center, axis=1, keepdims=True) + EPSILON)
    normal = center * inverse
    first_in = (normal * gain_one + shift_one).astype(jnp.bfloat16)
    second_in = (normal * gain_two + shift_two).astype(jnp.bfloat16)
    projected = jnp.dot(first_in, mixing_all, preferred_element_type=jnp.float32) + mixing_own
    expanded = jnp.dot(second_in, expand_all, preferred_element_type=jnp.float32) + expand_own
    local_heads = projected.shape[1] // (3 * HEAD_DIM)
    projected = projected.reshape(seq_len, local_heads, 3, HEAD_DIM)
    positions = jnp.arange(seq_len, dtype=jnp.int32)
    cosines, sine_values = rotary_tables(positions)
    queries = rotate(projected[:, :, 0], cosines, sine_values).astype(jnp.bfloat16)
    keys_all = rotate(projected[:, :, 1], cosines, sine_values).astype(jnp.bfloat16)
    values_all = projected[:, :, 2].astype(jnp.bfloat16)
    attended_grad = contract_cols(cotangent_all, output_all).astype(jnp.bfloat16)
    attended, query_grad, key_grad, value_grad = attention(
        queries, keys_all, values_all, attended_grad.reshape(seq_len, local_heads, HEAD_DIM)
    )
    activated_float, gelu_back = jax.vjp(exact_gelu, expanded)
    activated = activated_float.astype(jnp.bfloat16)
    branch = jnp.dot(attended, output_all, preferred_element_type=jnp.float32) + jnp.dot(
        activated, shrink_all, preferred_element_type=jnp.float32
    )
    summed = plane_scatter(branch, r, c)
    layer_out = (tokens.astype(jnp.float32) + summed + output_bias).astype(jnp.bfloat16)

    shrink_grad = contract_rows(activated, cotangent_all)
    shrink_sum = dp_scatter(shrink_grad.reshape(n_dp, unit, -1), n_dp, d)
    output_grad = contract_rows(attended, cotangent_all)
    output_mine = row_swap(
        output_grad.reshape(output_grad.shape[0], 4, -1).transpose(1, 0, 2), r
    )
    output_weight_grad = dp_scatter(
        output_mine.reshape(n_dp, -1, output_mine.shape[2]), n_dp, d
    )
    (expanded_float,) = gelu_back(contract_cols(cotangent_all, shrink_all))
    expanded_grad = expanded_float.astype(jnp.bfloat16)
    expand_grad = contract_rows(second_in, expanded_grad)
    depth = tokens.shape[1] // n_dp

    def by_dp(grad):
        return jnp.moveaxis(grad.reshape(4, n_dp, depth, -1), 1, 0)

    expand_sum = dp_scatter(by_dp(expand_grad), n_dp, d)

    query_grad = unrotate(query_grad, cosines, sine_values)
    key_grad = unrotate(key_grad, cosines, sine_values)
    projected_grad = jnp.stack([query_grad, key_grad, value_grad], axis=2).reshape(seq_len, -1)
    projected_grad = projected_grad.astype(jnp.bfloat16)
    mixing_grad = contract_rows(first_in, projected_grad)
    mixing_sum = dp_scatter(by_dp(mixing_grad), n_dp, d)
    first_part = contract_cols(projected_grad, mixing_all)
    second_part = contract_cols(expanded_grad, expand_all)
    normal_grad = plane_scatter(first_part * gain_one + second_part * gain_two, r, c)

    shrink_parts = shrink_sum.reshape(unit, 4, -1).transpose(1, 0, 2)
    packed = jnp.concatenate(
        [
            shrink_parts.reshape(4, -1, 128),
            expand_sum.reshape(4, -1, 128),
            mixing_sum.reshape(4, -1, 128),
        ],
        axis=1,
    )
    moved = row_swap(packed, r).astype(jnp.float32)
    cut_one = shrink_parts.size // 512
    cut_two = cut_one + expand_sum.size // 512
    shrink_weight_grad = moved[:, :cut_one].reshape(4 * unit, -1)
    expand_weight_grad = (
        moved[:, cut_one:cut_two]
        .reshape(4, depth, n_dp, unit)
        .transpose(1, 2, 0, 3)
        .reshape(depth, ff_block * 4)
    )
    mixing_weight_grad = (
        moved[:, cut_two:].reshape(4, depth, -1).transpose(1, 0, 2).reshape(depth, -1)
    )

    normal_cols = lax.dynamic_slice(
        normal,
        (c * tokens.shape[0], r * tokens.shape[1]),
        tokens.shape,
    )
    own_inverse = lax.dynamic_slice_in_dim(inverse, c * tokens.shape[0], tokens.shape[0], 0)
    sums = lax.psum(
        jnp.stack([jnp.sum(normal_grad, axis=1), jnp.sum(normal_grad * normal_cols, axis=1)]),
        "row",
    )
    tokens_grad = cotangent.astype(jnp.float32) + own_inverse * (
        normal_grad - sums[0][:, None] / D - normal_cols * (sums[1][:, None] / D)
    )

    shared = jnp.stack(
        [
            jnp.sum(first_part * normal, axis=0),
            jnp.sum(first_part, axis=0),
            jnp.sum(second_part * normal, axis=0),
            jnp.sum(second_part, axis=0),
        ]
    ).reshape(-1)
    bias_sum = jnp.sum(cotangent_all.astype(jnp.float32), axis=0)
    mixing_sums = jnp.sum(projected_grad.astype(jnp.float32), axis=0)
    expand_sums = jnp.sum(expanded_grad.astype(jnp.float32), axis=0)
    row_spot = jnp.arange(4) == r
    col_spot = jnp.arange(2) == c
    spot = (col_spot[:, None] & row_spot[None, :])[:, :, None]
    whole = jnp.concatenate(
        [
            shared,
            jnp.where((r == 0) & (c == 0), bias_sum, 0.0),
            jnp.where(spot, mixing_sums, 0.0).reshape(-1),
            jnp.where(spot, expand_sums, 0.0).reshape(-1),
        ]
    )
    whole = lax.psum(whole.reshape(-1, 128), ("dp", "row", "col")).reshape(-1)
    width = bias_sum.shape[0]
    small = whole[: 5 * width].reshape(5, 4 * n_dp, -1)
    small = take(small, r * n_dp + d, 1)
    mixing_end = 5 * width + 8 * mixing_sums.shape[0]
    mixing_bias_grad = take(whole[5 * width : mixing_end].reshape(2 * n_dp, -1), c * n_dp + d, 0)
    expand_all_bias = take(whole[mixing_end:].reshape(2, 4, n_dp, unit), c, 0)
    expand_bias_grad = take(expand_all_bias, d, 1).reshape(-1)
    return (
        layer_out,
        tokens_grad,
        small[0],
        small[1],
        small[2],
        small[3],
        mixing_weight_grad,
        mixing_bias_grad,
        output_weight_grad,
        expand_weight_grad,
        expand_bias_grad,
        shrink_weight_grad,
        small[4],
    )


def attention(queries, keys_all, values_all, attended_grad):
    seq_len = queries.shape[0]
    score_scale = 1.0 / math.sqrt(HEAD_DIM)
    positions = jnp.arange(seq_len, dtype=jnp.int32)
    causal = positions[:, None] >= positions[None, :]
    scores = (
        jnp.einsum("qhd,khd->hqk", queries, keys_all, preferred_element_type=jnp.float32)
        * score_scale
    )
    scores = jnp.where(causal[None], scores, NEGATIVE)
    row_peak = jnp.max(scores, axis=2, keepdims=True)
    powers = jnp.exp(scores - row_peak)
    soft_weights = powers / jnp.sum(powers, axis=2, keepdims=True)
    weights_low = soft_weights.astype(jnp.bfloat16)
    attended = jnp.einsum(
        "hqk,khd->qhd", weights_low, values_all, preferred_element_type=jnp.float32
    )
    attended = attended.astype(jnp.bfloat16).reshape(seq_len, -1)
    value_grad = jnp.einsum(
        "hqk,qhd->khd", weights_low, attended_grad, preferred_element_type=jnp.float32
    )
    prob_grad = jnp.einsum(
        "qhd,khd->hqk", attended_grad, values_all, preferred_element_type=jnp.float32
    )
    center_term = jnp.sum(soft_weights * prob_grad, axis=2, keepdims=True)
    score_grad = (soft_weights * (prob_grad - center_term)).astype(jnp.bfloat16)
    query_grad = (
        jnp.einsum("hqk,khd->qhd", score_grad, keys_all, preferred_element_type=jnp.float32)
        * score_scale
    )
    key_grad = (
        jnp.einsum("hqk,qhd->khd", score_grad, queries, preferred_element_type=jnp.float32)
        * score_scale
    )
    return attended, query_grad, key_grad, value_grad


def solution(mesh):
    placed = (
        P(("dp", "col"), "row"),
        P("row"),
        P("row"),
        P("row"),
        P("row"),
        P("row", "col"),
        P("col"),
        P("col", "row"),
        P("row", "col"),
        P("col"),
        P("col", "row"),
        P("row"),
        P(("dp", "col"), "row"),
    )
    return jax.shard_map(
        body,
        mesh=mesh,
        in_specs=placed,
        out_specs=(
            P(("dp", "col"), "row"),
            P(("dp", "col"), "row"),
            P(("row", "dp")),
            P(("row", "dp")),
            P(("row", "dp")),
            P(("row", "dp")),
            P(("row", "dp"), "col"),
            P(("col", "dp")),
            P(("col", "dp"), "row"),
            P(("row", "dp"), "col"),
            P(("col", "dp")),
            P(("col", "dp"), "row"),
            P(("row", "dp")),
        ),
        check_vma=False,
    )
```

```python
import functools
import math

import jax
import jax.numpy as jnp
from jax import lax
from jax.experimental import pallas as pl
from jax.experimental.pallas import tpu as pltpu
from jax.sharding import PartitionSpec as P

D = 1024
HEAD_DIM = 64
ROTARY = 16


EPSILON = 1e-05
NEGATIVE = -1e30


MESH = pl.DeviceIdType.MESH


def contract_rows(left_side, right_side):
    return lax.dot_general(
        left_side, right_side, (((0,), (0,)), ((), ())), preferred_element_type=jnp.float32
    )


def contract_cols(left_side, right_side):
    return lax.dot_general(
        left_side, right_side, (((1,), (1,)), ((), ())), preferred_element_type=jnp.float32
    )


def exact_gelu(values):
    return jax.nn.gelu(values, approximate=False)


def piece_of(ref, kind, index):
    if kind == "lanes":
        width = ref.shape[1] // 4
        return ref.at[:, pl.ds(pl.multiple_of(index * width, 128), width)]
    if kind == "whole":
        return ref
    return ref.at[index]


def place_of(ref, kind, index):
    if kind == "cols":
        width = ref.shape[1] // 4
        return ref.at[:, pl.ds(pl.multiple_of(index * width, 128), width)]
    height = ref.shape[0] // 4
    return ref.at[pl.ds(pl.multiple_of(index * height, 8), height)]


def exchange_kernel(n_gather, kinds, *refs):
    n_in = n_gather + len(kinds)
    begin_exchange(n_gather, kinds, refs[:n_in], refs[n_in : 2 * n_in], refs[2 * n_in :])()


def begin_exchange(n_gather, kinds, sources, targets, sems):
    n_in = n_gather + len(kinds)
    send_sems, recv_sems, own_sems = sems
    r, c = lax.axis_index("row"), lax.axis_index("col")
    across = lax.rem(r + 2, 4)
    mate = r + 1 - 2 * lax.rem(r, 2)
    other = 1 - c
    barrier = pltpu.get_barrier_semaphore()
    peers = [(lax.rem(r + s, 4), c) for s in (1, 2, 3)]
    if n_gather:
        peers += [(r, other), (across, other)]
    for row, col in peers:
        pl.semaphore_signal(
            barrier, inc=1, device_id={"row": row, "col": col}, device_id_type=MESH
        )
    pl.semaphore_wait(barrier, len(peers))

    counter = [0]

    def send(src, dst, row, col):
        k = counter[0]
        counter[0] += 1
        copy = pltpu.make_async_remote_copy(
            src_ref=src,
            dst_ref=dst,
            send_sem=send_sems.at[k],
            recv_sem=recv_sems.at[k],
            device_id={"row": row, "col": col},
            device_id_type=MESH,
        )
        copy.start()
        return copy

    def block_at(ref, row, col):
        height, width = ref.shape[0] // 2, ref.shape[1] // 4
        return ref.at[
            pl.ds(pl.multiple_of(col * height, 8), height),
            pl.ds(pl.multiple_of(row * width, 128), width),
        ]

    owns, first, rest = [], [], []
    for g in range(n_gather):
        for row, col in ((across, c), (r, other), (across, other)):
            first.append((g, row, col, send(sources[g], block_at(targets[g], r, c), row, col)))
    for g in range(n_gather):
        rest.append(send(sources[g], block_at(targets[g], r, c), mate, c))
    for t, kind in enumerate(kinds):
        for shift in (2, 3, 1):
            peer = lax.rem(r + shift, 4)
            rest.append(
                send(
                    piece_of(sources[n_gather + t], kind, peer),
                    place_of(targets[n_gather + t], kind, r),
                    peer,
                    c,
                )
            )
    for t in range(n_in):
        if t < n_gather:
            src, dst = sources[t], block_at(targets[t], r, c)
        else:
            kind = kinds[t - n_gather]
            src, dst = piece_of(sources[t], kind, r), place_of(targets[t], kind, r)
        copy = pltpu.make_async_copy(src, dst, own_sems.at[t])
        copy.start()
        owns.append(copy)

    def finish():
        for g, row, col, copy in first:
            copy.wait_recv()
            spot = block_at(targets[g], row, col)
            rest.append(send(spot, spot, mate, c))
        for g, row, col, copy in first:
            copy.wait_send()
        for copy in rest:
            copy.wait()
        for copy in owns:
            copy.wait()

    return finish


def landing(gathers, moves):
    outs = [jax.ShapeDtypeStruct((a.shape[0] * 2, a.shape[1] * 4), a.dtype) for a in gathers]
    for kind, a in moves:
        if kind == "lanes":
            shape = (a.shape[0] * 4, a.shape[1] // 4)
        elif kind == "whole":
            shape = (a.shape[0] * 4, a.shape[1])
        elif kind == "rows":
            shape = (a.shape[1] * 4, a.shape[2])
        else:
            shape = (a.shape[1], a.shape[2] * 4)
        outs.append(jax.ShapeDtypeStruct(shape, a.dtype))
    return outs


def exchange(gathers, moves, number):
    kinds = tuple(kind for kind, _ in moves)
    operands = tuple(gathers) + tuple(array for _, array in moves)
    outs = landing(gathers, moves)
    copies = 7 * len(gathers) + 3 * len(moves)
    return pl.pallas_call(
        functools.partial(exchange_kernel, len(gathers), kinds),
        out_shape=outs,
        in_specs=[pl.BlockSpec(memory_space=pltpu.VMEM)] * len(operands),
        out_specs=[pl.BlockSpec(memory_space=pltpu.VMEM)] * len(operands),
        scratch_shapes=[
            pltpu.SemaphoreType.DMA((copies,)),
            pltpu.SemaphoreType.DMA((copies,)),
            pltpu.SemaphoreType.DMA((len(operands),)),
        ],
        compiler_params=pltpu.CompilerParams(collective_id=number, has_side_effects=True),
    )(*operands)


def take(array, index, axis):
    return lax.dynamic_index_in_dim(array, index, axis, keepdims=False)


def scatter_kernel(count, *refs):
    parts, totals = refs[:count], refs[count : 2 * count]
    mate_in, low, far_in = refs[2 * count : 2 * count + 3]
    mate_send, mate_recv, far_send, far_recv = refs[2 * count + 3 :]
    r, c = lax.axis_index("row"), lax.axis_index("col")
    core, y = lax.rem(r, 2), r // 2
    across, mate, other = lax.rem(r + 2, 4), r + 1 - 2 * core, 1 - c
    half, width = totals[0].shape
    far = ((across, other), (across, c), (r, other))
    barrier = pltpu.get_barrier_semaphore()
    for row, col in ((mate, c),) + far:
        pl.semaphore_signal(
            barrier, inc=1, device_id={"row": row, "col": col}, device_id_type=MESH
        )
    pl.semaphore_wait(barrier, 4)

    def strip(row):
        return pl.ds(pl.multiple_of(row * width, 128), width)

    def half_of(col):
        return pl.ds(pl.multiple_of(col * half, 16), half)

    near = []
    for t in range(count):
        for k in range(2):
            copy = pltpu.make_async_remote_copy(
                src_ref=parts[t].at[:, strip(2 * k + 1 - core)],
                dst_ref=mate_in.at[t, k],
                send_sem=mate_send.at[2 * t + k],
                recv_sem=mate_recv.at[2 * t + k],
                device_id={"row": mate, "col": c},
                device_id_type=MESH,
            )
            copy.start()
            near.append(copy)
    sent = []
    for t in range(count):
        near[2 * t].wait_recv()
        near[2 * t + 1].wait_recv()
        for k, (row, col) in enumerate(far):
            rows, side = half_of(col), row // 2
            own = parts[t][rows, strip(row)].astype(jnp.float32)
            low[t, k] = (own + mate_in[t, side, rows, :].astype(jnp.float32)).astype(low.dtype)
            copy = pltpu.make_async_remote_copy(
                src_ref=low.at[t, k],
                dst_ref=far_in.at[t, k],
                send_sem=far_send.at[3 * t + k],
                recv_sem=far_recv.at[3 * t + k],
                device_id={"row": row, "col": col},
                device_id_type=MESH,
            )
            copy.start()
            sent.append(copy)
        rows = half_of(c)
        own = parts[t][rows, strip(r)].astype(jnp.float32)
        totals[t][...] = own + mate_in[t, y, rows, :].astype(jnp.float32)
    for t in range(count):
        for k in range(3):
            sent[3 * t + k].wait_recv()
            totals[t][...] += far_in[t, k].astype(jnp.float32)
    for copy in near + sent:
        copy.wait_send()


def plane_scatter(partials, number):
    count = len(partials)
    rows, cols = partials[0].shape
    half, width = rows // 2, cols // 4
    low = jnp.bfloat16
    return pl.pallas_call(
        functools.partial(scatter_kernel, count),
        out_shape=[jax.ShapeDtypeStruct((half, width), jnp.float32)] * count,
        in_specs=[pl.BlockSpec(memory_space=pltpu.VMEM)] * count,
        out_specs=[pl.BlockSpec(memory_space=pltpu.VMEM)] * count,
        scratch_shapes=[
            pltpu.VMEM((count, 2, rows, width), low),
            pltpu.VMEM((count, 3, half, width), low),
            pltpu.VMEM((count, 3, half, width), low),
            pltpu.SemaphoreType.DMA((2 * count,)),
            pltpu.SemaphoreType.DMA((2 * count,)),
            pltpu.SemaphoreType.DMA((3 * count,)),
            pltpu.SemaphoreType.DMA((3 * count,)),
        ],
        compiler_params=pltpu.CompilerParams(collective_id=number, has_side_effects=True),
    )(*[p.astype(low) for p in partials])


def take(array, index, axis):
    return lax.dynamic_index_in_dim(array, index, axis, keepdims=False)


def dp_scatter(chunks, n_dp, d):
    low = chunks.astype(jnp.bfloat16)
    if n_dp != 4:
        return lax.psum_scatter(low, "dp", scatter_dimension=0).astype(jnp.float32)
    low = low.reshape((2, 2) + low.shape[1:])
    came = lax.ppermute(take(low, 1 - d % 2, 1), "dp", [(i, i ^ 1) for i in range(4)])
    both = take(low, d % 2, 1).astype(jnp.float32) + came.astype(jnp.float32)
    sent = take(both, 1 - d // 2, 0).astype(jnp.bfloat16)
    came = lax.ppermute(sent, "dp", [(i, i ^ 2) for i in range(4)])
    return take(both, d // 2, 0) + came.astype(jnp.float32)


def dp_total(vector, n_dp):
    if n_dp != 4:
        return lax.psum(vector, "dp")
    for bit in (1, 2):
        vector = vector + lax.ppermute(vector, "dp", [(i, i ^ bit) for i in range(4)])
    return vector


def row_swap(chunks, r):
    low = chunks.astype(jnp.bfloat16)
    result = low
    for shift in (1, 2, 3):
        sent = take(low, (r + shift) % 4, 0)
        came = lax.ppermute(sent, "row", [(i, (i + shift) % 4) for i in range(4)])
        result = lax.dynamic_update_index_in_dim(result, came, (r - shift) % 4, 0)
    return result


def body(
    tokens,
    first_gain,
    first_shift,
    second_gain,
    second_shift,
    mixing_weight,
    mixing_bias,
    output_weight,
    expand_weight,
    expand_bias,
    shrink_weight,
    output_bias,
    cotangent,
):
    n_dp = lax.axis_size("dp")
    d, r, c = lax.axis_index("dp"), lax.axis_index("row"), lax.axis_index("col")
    ff_block = expand_weight.shape[1] // 4
    unit = ff_block // n_dp

    def by_unit(array, axis):
        dims = array.shape
        split = array.reshape(dims[:axis] + (n_dp, 4, unit) + dims[axis + 1 :])
        moved = jnp.moveaxis(split, axis + 1, 0)
        return moved.reshape((4,) + dims[:axis] + (ff_block,) + dims[axis + 1 :])

    vectors = jnp.stack([first_gain, first_shift, second_gain, second_shift])
    vectors = jnp.concatenate([vectors, jnp.zeros_like(vectors)])
    tokens_all, cotangent_all, mixing_all, vectors_all, output_all = exchange(
        [tokens, cotangent],
        [
            ("lanes", mixing_weight),
            ("whole", vectors),
            ("cols", output_weight.reshape(4, -1, output_weight.shape[1])),
        ],
        0,
    )
    vectors_all = vectors_all.reshape(4, 8, -1).transpose(1, 0, 2).reshape(8, -1)
    gain_one, shift_one, gain_two, shift_two = (vectors_all[i] for i in range(4))
    mixing_own = take(mixing_bias.reshape(4, -1), r, 0)
    expand_own = take(by_unit(expand_bias, 0), r, 0)

    seq_len = tokens_all.shape[0]
    floats = tokens_all.astype(jnp.float32)
    center = floats - jnp.mean(floats, axis=1, keepdims=True)
    inverse = lax.rsqrt(jnp.mean(center * center, axis=1, keepdims=True) + EPSILON)
    normal = center * inverse
    first_in = (normal * gain_one + shift_one).astype(jnp.bfloat16)
    second_in = (normal * gain_two + shift_two).astype(jnp.bfloat16)
    projected = jnp.dot(first_in, mixing_all, preferred_element_type=jnp.float32) + mixing_own
    attended_grad = contract_cols(cotangent_all, output_all).astype(jnp.bfloat16)
    attended, projected_grad, expand_all, shrink_all = attention(
        projected,
        attended_grad,
        [("rows", by_unit(expand_weight, 1)), ("cols", by_unit(shrink_weight, 0))],
        1,
    )
    expanded = jnp.dot(second_in, expand_all, preferred_element_type=jnp.float32) + expand_own
    activated_float, gelu_back = jax.vjp(exact_gelu, expanded)
    activated = activated_float.astype(jnp.bfloat16)
    branch = jnp.dot(attended, output_all, preferred_element_type=jnp.float32) + jnp.dot(
        activated, shrink_all, preferred_element_type=jnp.float32
    )
    shrink_grad = contract_rows(activated, cotangent_all)
    shrink_sum = dp_scatter(shrink_grad.reshape(n_dp, unit, -1), n_dp, d)
    output_grad = contract_rows(attended, cotangent_all)
    output_mine = row_swap(
        output_grad.reshape(output_grad.shape[0], 4, -1).transpose(1, 0, 2), r
    )
    output_weight_grad = dp_scatter(
        output_mine.reshape(n_dp, -1, output_mine.shape[2]), n_dp, d
    )
    (expanded_float,) = gelu_back(contract_cols(cotangent_all, shrink_all))
    expanded_grad = expanded_float.astype(jnp.bfloat16)
    expand_grad = contract_rows(second_in, expanded_grad)
    depth = tokens.shape[1] // n_dp

    def by_dp(grad):
        return jnp.moveaxis(grad.reshape(4, n_dp, depth, -1), 1, 0)

    expand_sum = dp_scatter(by_dp(expand_grad), n_dp, d)

    mixing_grad = contract_rows(first_in, projected_grad)
    mixing_sum = dp_scatter(by_dp(mixing_grad), n_dp, d)
    first_part = contract_cols(projected_grad, mixing_all)
    second_part = contract_cols(expanded_grad, expand_all)
    summed, normal_grad = plane_scatter(
        [branch, first_part * gain_one + second_part * gain_two], 2
    )
    layer_out = (tokens.astype(jnp.float32) + summed + output_bias).astype(jnp.bfloat16)

    shrink_parts = shrink_sum.reshape(unit, 4, -1).transpose(1, 0, 2)
    packed = jnp.concatenate(
        [
            shrink_parts.reshape(4, -1, 128),
            expand_sum.reshape(4, -1, 128),
            mixing_sum.reshape(4, -1, 128),
        ],
        axis=1,
    )
    normal_cols = lax.dynamic_slice(
        normal,
        (c * tokens.shape[0], r * tokens.shape[1]),
        tokens.shape,
    )
    shared = jnp.stack(
        [
            jnp.sum(first_part * normal, axis=0),
            jnp.sum(first_part, axis=0),
            jnp.sum(second_part * normal, axis=0),
            jnp.sum(second_part, axis=0),
        ]
    ).reshape(-1)
    bias_sum = jnp.sum(cotangent_all.astype(jnp.float32), axis=0)
    mixing_sums = jnp.sum(projected_grad.astype(jnp.float32), axis=0)
    expand_sums = jnp.sum(expanded_grad.astype(jnp.float32), axis=0)
    local = jnp.concatenate([shared, bias_sum, mixing_sums, expand_sums]).reshape(-1, 128)
    local = dp_total(local, n_dp)
    twin = lax.ppermute(local, "col", [(0, 1), (1, 0)])
    n_shared = shared.shape[0] // 128
    local = jnp.concatenate([local[:n_shared] + twin[:n_shared], local[n_shared:]])
    local = jnp.pad(local, ((0, -local.shape[0] % 8), (0, 0)))
    own_sums = jnp.stack(
        [jnp.sum(normal_grad, axis=1), jnp.sum(normal_grad * normal_cols, axis=1)]
    )
    own_sums = jnp.pad(own_sums, ((0, 6), (0, 0)))
    moved, locals_all, sums = exchange(
        [],
        [("rows", packed.astype(jnp.bfloat16)), ("whole", local), ("whole", own_sums)],
        3,
    )
    moved = moved.reshape(packed.shape).astype(jnp.float32)
    locals_all = locals_all.reshape(4, -1)
    sums = jnp.sum(sums.reshape(4, 8, -1)[:, :2], axis=0)
    cut_one = shrink_parts.size // 512
    cut_two = cut_one + expand_sum.size // 512
    shrink_weight_grad = moved[:, :cut_one].reshape(4 * unit, -1)
    expand_weight_grad = (
        moved[:, cut_one:cut_two]
        .reshape(4, depth, n_dp, unit)
        .transpose(1, 2, 0, 3)
        .reshape(depth, ff_block * 4)
    )
    mixing_weight_grad = (
        moved[:, cut_two:].reshape(4, depth, -1).transpose(1, 0, 2).reshape(depth, -1)
    )

    own_inverse = lax.dynamic_slice_in_dim(inverse, c * tokens.shape[0], tokens.shape[0], 0)
    tokens_grad = cotangent.astype(jnp.float32) + own_inverse * (
        normal_grad - sums[0][:, None] / D - normal_cols * (sums[1][:, None] / D)
    )

    width = bias_sum.shape[0]
    n_mixing = mixing_sums.shape[0]
    shared_all = jnp.sum(locals_all[:, : 4 * width], axis=0).reshape(4, 4 * n_dp, -1)
    shared_all = take(shared_all, r * n_dp + d, 1)
    bias_all = take(locals_all[0, 4 * width : 5 * width].reshape(4 * n_dp, -1), r * n_dp + d, 0)
    mixing_part = locals_all[:, 5 * width : 5 * width + n_mixing]
    mixing_bias_grad = take(mixing_part.reshape(n_dp, -1), d, 0)
    expand_part = locals_all[:, 5 * width + n_mixing :][:, :ff_block]
    expand_bias_grad = take(expand_part.reshape(4, n_dp, unit), d, 1).reshape(-1)
    return (
        layer_out,
        tokens_grad,
        shared_all[0],
        shared_all[1],
        shared_all[2],
        shared_all[3],
        mixing_weight_grad,
        mixing_bias_grad,
        output_weight_grad,
        expand_weight_grad,
        expand_bias_grad,
        shrink_weight_grad,
        bias_all,
    )


def turn(block, stay, after, before):
    width = block.shape[1]
    return (
        block * stay
        + pltpu.roll(block, width - ROTARY // 2, 1) * after
        + pltpu.roll(block, ROTARY // 2, 1) * before
    )


def attention_kernel(kinds, *refs):
    n_moves = len(kinds)
    projected, out_grad, stay, after, before = refs[:5]
    sources, refs = refs[5 : 5 + n_moves], refs[5 + n_moves :]
    attended, projected_grad = refs[:2]
    targets, refs = refs[2 : 2 + n_moves], refs[2 + n_moves :]
    queries, keys, values, value_rows, query_acc, key_acc, value_acc = refs[:7]
    finish = begin_exchange(0, kinds, sources, targets, refs[7:])
    seq_len = projected.shape[0]
    heads = projected.shape[1] // (3 * HEAD_DIM)
    block = 256
    steps = seq_len // block
    score_scale = 1.0 / math.sqrt(HEAD_DIM)

    @pl.loop(0, steps)
    def _(step):
        rows = pl.ds(pl.multiple_of(step * block, block), block)
        turned = turn(projected[rows, :], stay[rows, :], after[rows, :], before[rows, :])
        turned = turned.astype(jnp.bfloat16)
        given = out_grad[rows, :]
        for h in range(heads):
            base = 3 * HEAD_DIM * h
            queries[h, rows, :] = turned[:, base : base + HEAD_DIM]
            keys[h, rows, :] = turned[:, base + HEAD_DIM : base + 2 * HEAD_DIM]
            values[h, rows, :] = turned[:, base + 2 * HEAD_DIM : base + 3 * HEAD_DIM]
            value_rows[h, rows, :] = given[:, h * HEAD_DIM : (h + 1) * HEAD_DIM]

    parts = []
    for h in range(heads):
        parts.append([])
        for step in range(steps):
            low, high = step * block, (step + 1) * block
            query, given = queries[h, low:high, :], value_rows[h, low:high, :]
            key, value = keys[h, :high, :], values[h, :high, :]
            scores = contract_cols(query, key) * score_scale
            row_at = low + lax.broadcasted_iota(jnp.int32, scores.shape, 0)
            col_at = lax.broadcasted_iota(jnp.int32, scores.shape, 1)
            scores = jnp.where(row_at >= col_at, scores, NEGATIVE)
            powers = jnp.exp(scores - jnp.max(scores, axis=1, keepdims=True))
            soft = powers / jnp.sum(powers, axis=1, keepdims=True)
            soft_low = soft.astype(jnp.bfloat16)
            parts[h].append(jnp.dot(soft_low, value, preferred_element_type=jnp.float32))
            prob_grad = contract_cols(given, value)
            middle = jnp.sum(soft * prob_grad, axis=1, keepdims=True)
            score_grad = (soft * (prob_grad - middle)).astype(jnp.bfloat16)
            query_acc[h, low:high, :] = (
                jnp.dot(score_grad, key, preferred_element_type=jnp.float32) * score_scale
            )
            key_part = contract_rows(score_grad, query) * score_scale
            value_part = contract_rows(soft_low, given)
            if step:
                key_acc[h, :low, :] += key_part[:low]
                value_acc[h, :low, :] += value_part[:low]
            key_acc[h, low:high, :] = key_part[low:]
            value_acc[h, low:high, :] = value_part[low:]
    for step in range(steps):
        attended[step * block : (step + 1) * block, :] = jnp.concatenate(
            [parts[h][step].astype(jnp.bfloat16) for h in range(heads)], axis=1
        )

    @pl.loop(0, steps)
    def _(step):
        rows = pl.ds(pl.multiple_of(step * block, block), block)
        pieces = []
        for h in range(heads):
            pieces += [query_acc[h, rows, :], key_acc[h, rows, :], value_acc[h, rows, :]]
        joined = jnp.concatenate(pieces, axis=1)
        joined = turn(joined, stay[rows, :], -after[rows, :], -before[rows, :])
        projected_grad[rows, :] = joined.astype(jnp.bfloat16)

    finish()


def lane_tables(seq_len, heads):
    half = ROTARY // 2
    lane = jnp.arange(3 * HEAD_DIM * heads, dtype=jnp.int32) % (3 * HEAD_DIM)
    inner = lane % HEAD_DIM
    turns = (lane < 2 * HEAD_DIM) & (inner < ROTARY)
    ladder = (inner % half).astype(jnp.float32)
    rates = 1.0 / 10000.0 ** (2.0 * ladder / ROTARY)
    angles = jnp.arange(seq_len, dtype=jnp.int32).astype(jnp.float32)[:, None] * rates[None, :]
    cosines, sines = jnp.cos(angles), jnp.sin(angles)
    stay = jnp.where(turns[None], cosines, 1.0)
    after = jnp.where((turns & (inner < half))[None], -sines, 0.0)
    before = jnp.where((turns & (inner >= half))[None], sines, 0.0)
    return stay, after, before


def attention(projected, out_grad, moves, number):
    seq_len = projected.shape[0]
    heads = projected.shape[1] // (3 * HEAD_DIM)
    stay, after, before = lane_tables(seq_len, heads)
    lows = pltpu.VMEM((heads, seq_len, HEAD_DIM), jnp.bfloat16)
    sums = pltpu.VMEM((heads, seq_len, HEAD_DIM), jnp.float32)
    work = seq_len * seq_len * heads
    return pl.pallas_call(
        functools.partial(attention_kernel, tuple(kind for kind, _ in moves)),
        out_shape=[
            jax.ShapeDtypeStruct((seq_len, heads * HEAD_DIM), jnp.bfloat16),
            jax.ShapeDtypeStruct(projected.shape, jnp.bfloat16),
        ]
        + landing([], moves),
        in_specs=[pl.BlockSpec(memory_space=pltpu.VMEM)] * (5 + len(moves)),
        out_specs=[pl.BlockSpec(memory_space=pltpu.VMEM)] * (2 + len(moves)),
        scratch_shapes=[lows] * 4
        + [sums] * 3
        + [
            pltpu.SemaphoreType.DMA((3 * len(moves),)),
            pltpu.SemaphoreType.DMA((3 * len(moves),)),
            pltpu.SemaphoreType.DMA((len(moves),)),
        ],
        compiler_params=pltpu.CompilerParams(collective_id=number, has_side_effects=True),
        cost_estimate=pl.CostEstimate(
            flops=work * HEAD_DIM * 14, bytes_accessed=8 * projected.size, transcendentals=work
        ),
    )(projected, out_grad, stay, after, before, *[array for _, array in moves])


def solution(mesh):
    placed = (
        P(("dp", "col"), "row"),
        P("row"),
        P("row"),
        P("row"),
        P("row"),
        P("row", "col"),
        P("col"),
        P("col", "row"),
        P("row", "col"),
        P("col"),
        P("col", "row"),
        P("row"),
        P(("dp", "col"), "row"),
    )
    return jax.shard_map(
        body,
        mesh=mesh,
        in_specs=placed,
        out_specs=(
            P(("dp", "col"), "row"),
            P(("dp", "col"), "row"),
            P(("row", "dp")),
            P(("row", "dp")),
            P(("row", "dp")),
            P(("row", "dp")),
            P(("row", "dp"), "col"),
            P(("col", "dp")),
            P(("col", "dp"), "row"),
            P(("row", "dp"), "col"),
            P(("col", "dp")),
            P(("col", "dp"), "row"),
            P(("row", "dp")),
        ),
        check_vma=False,
    )
```
